128 devices in a mesh: dp: 4 (over y), region: 32 (over x, z, core).
Axes of the slice: x: 4, y: 4, z: 4, core: 2. Of those that a mesh axis runs over, the one named last changes fastest.
Arguments:
- leaves: float32 [512, 64, 1024], P('region', None, 'dp'), may hold values from -280 to 0
- weights: float32 [2, 512, 8, 64, 64], P(None, 'region'), may hold values from 0.00048828125 to 0.0078125
- groups: int32 [2, 32, 32, 2], P(None, None, 'region'), may hold values from 0 to 15
- prod_kids: int32 [2, 1024, 2], P(None, 'region'), may hold values from 0 to 63
- sum_kids: int32 [2, 512, 8], P(None, 'region'), may hold values from 0 to 31
- cotangent: float32 [512, 64, 1024], P('region', None, 'dp'), may hold values from -6 to 6
Outputs:
- top_logp: float32 [512, 64, 1024], P('region', None, 'dp')
- leaf_grad: float32 [512, 64, 1024], P('region', None, 'dp')
- weight_flow: float32 [2, 512, 8, 64, 64], P(None, 'region')
The draws below stay inside these ranges and needn't reach their ends.
All inputs are finite; a program needn't handle non-finite values.
Results may differ from the reference program's by a relative error of at most 0.0003.
Values sent between devices are 32-bit elements; how exact they have to be, the bound alone decides.
No kernel may reach another device: no remote copies, remote signals or barrier semaphores. Data moves between devices by JAX's collectives and lax.ppermute only.
A program may use at most 128 MiB of HBM per device.

```python
import math
import jax
import jax.numpy as jnp
from jax import lax

BLOCK = 64
B_DEV = 16
K = 8
G = 2
PAIRS = 2
P_DEV = 32
SLOTS = 64
NBLK = 512
SAMPLES = 1024
N_REGION = 32


def draw_leaves(key, part):
    second = jax.random.fold_in(key, 1)
    shape = (NBLK, BLOCK, SAMPLES)
    values = -6.0 * jax.random.uniform(second, shape, jnp.float32)
    return values.astype(jnp.float32)


def set_ends(array, key, smallest, top_value):
    index_at = [jax.random.randint(jax.random.fold_in(key, axis), (), 0, length) for axis, length in enumerate(array.shape)]
    widest = array.shape.index(max(array.shape))
    beside = index_at[:widest] + [(index_at[widest] + 1) % array.shape[widest]] + index_at[widest + 1:]
    return array.at[tuple(index_at)].set(smallest).at[tuple(beside)].set(top_value)


def level_of(stream_key, shape, shards, low, high):
    factor_of = 1.0
    for axis_at, shards_of in shards:
        heights = jax.random.uniform(jax.random.fold_in(jax.random.fold_in(stream_key, 6), axis_at), (shards_of,), jnp.float32, low / len(shards), high / len(shards))
        factor_of = factor_of * jnp.repeat(jnp.exp(heights), shape[axis_at] // shards_of).reshape((-1,) + (1,) * (len(shape) - 1 - axis_at))
    return factor_of


def noise(rng, dims, spread, limit, cuts=(), kind=jnp.bfloat16):
    result = spread * jax.random.normal(rng, dims, jnp.float32)
    if cuts:
        result = result * level_of(rng, dims, cuts, -0.22, 0.18)
    return jnp.clip(result, -limit, limit).astype(kind)


def setup_inputs(seed: int = 0) -> dict:
    keys = jax.random.split(jax.random.key(seed), 7)
    return {
        "leaves": draw_leaves(jax.random.fold_in(keys[6], 71), 0),
        "weights": jnp.clip(jnp.exp(math.log(0.0078125) - 2.7725887 * jax.random.uniform(keys[1], (PAIRS, NBLK, K, BLOCK, BLOCK), jnp.float32) ** level_of(keys[1], (PAIRS, NBLK, K, BLOCK, BLOCK), ((1, 32),), -0.2, 0.2)), 0.00048828125, 0.0078125),
        "groups": set_ends(jax.random.randint(keys[2], (PAIRS, N_REGION, N_REGION, G), 0, B_DEV), jax.random.fold_in(keys[2], 1), 0, B_DEV - 1).astype(jnp.int32),
        "prod_kids": set_ends(jax.random.randint(keys[3], (PAIRS, N_REGION * P_DEV, 2), 0, SLOTS), jax.random.fold_in(keys[3], 1), 0, SLOTS - 1).astype(jnp.int32),
        "sum_kids": set_ends(jax.random.randint(keys[4], (PAIRS, NBLK, K), 0, P_DEV), jax.random.fold_in(keys[4], 1), 0, P_DEV - 1).astype(jnp.int32),
        "cotangent": noise(keys[5], (NBLK, BLOCK, SAMPLES), 1.0, 6.0, ((0, 32), (2, 4)), jnp.float32),
    }


def reader_layer(level_in, slot_src, kid_pairs, sum_list, weight_part):
    gathered = level_in[slot_src]
    prods = gathered[kid_pairs[:, 0]] + gathered[kid_pairs[:, 1]]
    chosen = prods[sum_list]
    shift_top = lax.stop_gradient(lax.optimization_barrier(jnp.max(chosen, axis=(1, 2), keepdims=True)))
    exponent = jnp.exp(chosen - shift_top)
    running_totals = jnp.einsum('bkij,bkjs->bis', weight_part, exponent, precision=lax.Precision.HIGHEST)
    return shift_top[:, 0] + jnp.log(running_totals)

def layer(level_in, group_ids, kid_all, sum_all, weight_complete):
    source_offset = (jnp.arange(N_REGION, dtype=jnp.int32) * B_DEV)[None, :, None]
    slot_src = (group_ids + source_offset).reshape(N_REGION, SLOTS).astype(jnp.int32)

    def stepper(items):
        return reader_layer(level_in, items[0], items[1], items[2], items[3])
    outputs = lax.map(jax.checkpoint(stepper), (slot_src, kid_all.reshape(N_REGION, P_DEV, 2), sum_all.reshape(N_REGION, B_DEV, K), weight_complete.reshape(N_REGION, B_DEV, K, BLOCK, BLOCK)))
    return outputs.reshape(NBLK, BLOCK, SAMPLES)

def reference(leaves, weights, groups, prod_kids, sum_kids, cotangent):

    def forward(level_in, weight_complete):
        for level in range(PAIRS):
            level_in = layer(level_in, groups[level], prod_kids[level], sum_kids[level], weight_complete[level])
        return level_in
    top_logp, pullback = jax.vjp(forward, leaves, weights)
    leaf_grad, weight_grad = pullback(cotangent)
    return (top_logp, leaf_grad, weight_grad / SAMPLES)
```

```python
import functools

import jax
import jax.numpy as jnp
from jax import lax
from jax.experimental import pallas as pl
from jax.experimental.pallas import tpu as pltpu
from jax.sharding import PartitionSpec as P

F32 = jnp.float32
BF16 = jnp.bfloat16
ANY = pl.BlockSpec(memory_space=pl.ANY)
SMEM = pl.BlockSpec(memory_space=pltpu.SMEM)


def whole(shape):
    return pl.BlockSpec(shape, lambda i: (0,) * len(shape))


def cost(flops, touched):
    return pl.CostEstimate(flops=flops, bytes_accessed=touched, transcendentals=0)


def split(x):
    high = x.astype(BF16)
    return high, (x - high.astype(F32)).astype(BF16)


def prepare_kernel(w_ref, wf_ref, wt_ref):
    kids = w_ref.shape[2]
    wide = jnp.concatenate([w_ref[0, 0, k] for k in range(kids)], axis=1)
    high = wide.astype(BF16)
    low = (wide - high.astype(F32)).astype(BF16)
    stacked = jnp.concatenate([high, low], axis=0)
    wf_ref[0, 0] = stacked
    both = jnp.concatenate([high.astype(F32), low.astype(F32)], axis=0)
    wt_ref[0, 0] = both.T.astype(BF16)


def prepare(weights):
    levels, blocks, kids, n, _ = weights.shape
    return pl.pallas_call(
        prepare_kernel,
        grid=(levels, blocks),
        in_specs=[pl.BlockSpec((1, 1, kids, n, n), lambda l, b: (l, b, 0, 0, 0))],
        out_specs=[
            pl.BlockSpec((1, 1, 2 * n, kids * n), lambda l, b: (l, b, 0, 0)),
            pl.BlockSpec((1, 1, kids * n, 2 * n), lambda l, b: (l, b, 0, 0)),
        ],
        out_shape=[
            jax.ShapeDtypeStruct((levels, blocks, 2 * n, kids * n), BF16),
            jax.ShapeDtypeStruct((levels, blocks, kids * n, 2 * n), BF16),
        ],
        name="prepare",
        cost_estimate=cost(0, 20 << 20),
    )(weights)


def send_slots(ids_ref, source, out_ref, sem):
    count = out_ref.shape[0]

    def start(t, carry):
        pltpu.make_async_copy(source.at[ids_ref[t]], out_ref.at[t], sem.at[t]).start()
        return carry

    def finish(t, carry):
        pltpu.make_async_copy(source.at[0], out_ref.at[t], sem.at[t]).wait()
        return carry

    lax.fori_loop(0, count, start, 0)
    lax.fori_loop(0, count, finish, 0)


def take_kernel(ids_ref, leaves_ref, out_ref, sem):
    send_slots(ids_ref, leaves_ref, out_ref, sem)


def take(ids, leaves, chunk, s):
    blocks, n, _ = leaves.shape
    slots = ids.shape[0]
    return pl.pallas_call(
        take_kernel,
        grid=(1,),
        in_specs=[SMEM, pl.BlockSpec((blocks, n, s), lambda i: (0, 0, chunk))],
        out_specs=ANY,
        out_shape=jax.ShapeDtypeStruct((slots, n, s), F32),
        scratch_shapes=[pltpu.SemaphoreType.DMA((slots,))],
        name="take",
        cost_estimate=cost(0, 6 << 20),
    )(ids, leaves)


def make_products(kids_ref, recv_ref, e_ref, m_ref):
    n, s = recv_ref.shape[1:]

    def body(p, carry):
        prod = recv_ref[kids_ref[2 * p]] + recv_ref[kids_ref[2 * p + 1]]
        top = jnp.broadcast_to(jnp.max(prod, axis=0, keepdims=True), (8, s))
        m_ref[p] = top
        e_ref[p] = jnp.exp(prod.reshape(n // 8, 8, s) - top[None]).reshape(n, s)
        return carry

    lax.fori_loop(0, e_ref.shape[0], body, 0, unroll=2)


def scales(sums_ref, b, kids, m_ref):
    tops = [m_ref[sums_ref[b * kids + k]] for k in range(kids)]
    shift = functools.reduce(jnp.maximum, tops)
    return shift, [jnp.exp(t - shift) for t in tops]


def fill_terms(sums_ref, b, kids, e_ref, factors, x_ref):
    n, s = e_ref.shape[1:]
    for k in range(kids):
        e = e_ref[sums_ref[b * kids + k]]
        high, low = split((e.reshape(n // 8, 8, s) * factors[k][None]).reshape(n, s))
        x_ref[pl.ds(k * n, n), pl.ds(0, s)] = high
        x_ref[pl.ds(k * n, n), pl.ds(s, s)] = low


def sum_terms(wf, x_ref, n, s):
    both = jnp.dot(wf, x_ref[...], preferred_element_type=F32)
    return (both[:n, :s] + (both[n:, :s] + both[:n, s:])) + both[n:, s:]


def add_shift(shift, totals):
    n, s = totals.shape
    return (jnp.log(totals).reshape(n // 8, 8, s) + shift[None]).reshape(n, s)


def weight_terms(r_high, r_low, x_ref, s):
    dims = (((1,), (1,)), ((), ()))
    main = lax.dot_general(
        jnp.concatenate([r_high, r_high], axis=1), x_ref[...], dims, preferred_element_type=F32
    )
    return main + lax.dot_general(
        r_low, x_ref[:, pl.ds(0, s)], dims, preferred_element_type=F32
    )


def child_terms(wt, r_high, r_low, sums_ref, b, kids, factors, g_ref):
    n, s = r_high.shape
    right = jnp.concatenate([r_high, r_high, r_low, r_low], axis=0)
    y = jnp.dot(jnp.concatenate([wt, wt], axis=1), right, preferred_element_type=F32)
    for k in range(kids):
        p = sums_ref[b * kids + k]
        part = y[k * n : (k + 1) * n].reshape(n // 8, 8, s) * factors[k][None]
        g_ref[p] = g_ref[p] + part.reshape(n, s)


def slot_terms(kids_ref, e_ref, g_ref, out_ref):
    out_ref[...] = jnp.zeros_like(out_ref)

    def body(p, carry):
        g = g_ref[p] * e_ref[p]
        first, second = kids_ref[2 * p], kids_ref[2 * p + 1]
        out_ref[first] = out_ref[first] + g
        out_ref[second] = out_ref[second] + g
        return carry

    lax.fori_loop(0, e_ref.shape[0], body, 0)


def home_sums(ids_ref, recv_ref, acc_ref):
    acc_ref[...] = jnp.zeros_like(acc_ref)

    def body(t, carry):
        b = ids_ref[t]
        acc_ref[b] = acc_ref[b] + recv_ref[t]
        return carry

    lax.fori_loop(0, recv_ref.shape[0], body, 0)


def forward_kernel(kids, kids_ref, sums_ref, next_ref, recv_ref, wf_ref, out_ref, e_ref, m_ref, tot_ref, lv_ref, x_ref, sem):
    n, s = recv_ref.shape[1:]
    make_products(kids_ref, recv_ref, e_ref, m_ref)

    def body(b, carry):
        shift, factors = scales(sums_ref, b, kids, m_ref)
        fill_terms(sums_ref, b, kids, e_ref, factors, x_ref)
        totals = sum_terms(wf_ref[0, b], x_ref, n, s)
        tot_ref[b] = totals
        lv_ref[b] = add_shift(shift, totals)
        return carry

    lax.fori_loop(0, lv_ref.shape[0], body, 0)
    send_slots(next_ref, lv_ref, out_ref, sem)


def forward_layer(layer, kids_ids, sum_ids, next_ids, recv, wf):
    slots, n, s = recv.shape
    blocks, _, wide = wf.shape[1:]
    kids = wide // n
    prods = kids_ids.shape[0] // 2
    return pl.pallas_call(
        functools.partial(forward_kernel, kids),
        grid=(1,),
        in_specs=[
            SMEM,
            SMEM,
            SMEM,
            whole((slots, n, s)),
            pl.BlockSpec((1, blocks, 2 * n, wide), lambda i: (layer, 0, 0, 0)),
        ],
        out_specs=[ANY, whole((prods, n, s)), whole((prods, 8, s)), whole((blocks, n, s))],
        out_shape=[
            jax.ShapeDtypeStruct((slots, n, s), F32),
            jax.ShapeDtypeStruct((prods, n, s), F32),
            jax.ShapeDtypeStruct((prods, 8, s), F32),
            jax.ShapeDtypeStruct((blocks, n, s), F32),
        ],
        scratch_shapes=[
            pltpu.VMEM((blocks, n, s), F32),
            pltpu.VMEM((wide, 2 * s), BF16),
            pltpu.SemaphoreType.DMA((slots,)),
        ],
        name="forward",
        cost_estimate=cost(2 * blocks * 2 * n * wide * 2 * s, 10 << 20),
    )(kids_ids, sum_ids, next_ids, recv, wf)


def put_flow(flow_ref, outs, sem):
    if len(outs) == 1:
        return
    part = flow_ref.shape[0] // len(outs)
    copies = [
        pltpu.make_async_copy(flow_ref.at[pl.ds(j * part, part)], out, sem.at[j])
        for j, out in enumerate(outs)
    ]
    for copy in copies:
        copy.start()
    for copy in copies:
        copy.wait()


def middle_kernel(kids, last, me_ref, kids_ref, sums_ref, recv_ref, cot_ref, wf_ref, wt_ref, *refs):
    if last:
        _, before_ref, top_ref, sg_ref, f0, f1, f2, f3, e_ref, m_ref, g_ref, x_ref, flow_ref, sem = refs
    else:
        top_ref, sg_ref, flow_ref, e_ref, m_ref, g_ref, x_ref = refs
    n, s = recv_ref.shape[1:]
    blocks = cot_ref.shape[0]
    make_products(kids_ref, recv_ref, e_ref, m_ref)
    g_ref[...] = jnp.zeros_like(g_ref)

    def body(at, carry):
        b = lax.rem(at + me_ref[0], blocks)
        shift, factors = scales(sums_ref, b, kids, m_ref)
        fill_terms(sums_ref, b, kids, e_ref, factors, x_ref)
        totals = sum_terms(wf_ref[0, b], x_ref, n, s)
        top_ref[b] = add_shift(shift, totals)
        r_high, r_low = split(cot_ref[b] / totals)
        flow = weight_terms(r_high, r_low, x_ref, s)
        flow_ref[at] = flow + before_ref[at] if last else flow
        child_terms(wt_ref[0, b], r_high, r_low, sums_ref, b, kids, factors, g_ref)
        return carry

    lax.fori_loop(0, blocks, body, 0)
    if last:
        part = blocks // 4
        outs = (f0, f1, f2, f3)
        for j in range(4):
            pltpu.make_async_copy(flow_ref.at[pl.ds(j * part, part)], outs[j], sem.at[j]).start()
    slot_terms(kids_ref, e_ref, g_ref, sg_ref)
    if last:
        for j in range(4):
            pltpu.make_async_copy(flow_ref.at[pl.ds(j * part, part)], outs[j], sem.at[j]).wait()


def middle_layer(layer, chunk, me, kids_ids, sum_ids, recv, cot, wf, wt, top=None, before=None):
    slots, n, s = recv.shape
    blocks, _, wide = wf.shape[1:]
    kids = wide // n
    prods = kids_ids.shape[0] // 2
    last = before is not None
    in_specs = [
        SMEM,
        SMEM,
        SMEM,
        whole((slots, n, s)),
        pl.BlockSpec((blocks, n, s), lambda i: (0, 0, chunk)),
        pl.BlockSpec((1, blocks, 2 * n, wide), lambda i: (layer, 0, 0, 0)),
        pl.BlockSpec((1, blocks, wide, 2 * n), lambda i: (layer, 0, 0, 0)),
    ]
    args = [me, kids_ids, sum_ids, recv, cot, wf, wt]
    flow_shape = (blocks, n, wide)
    part_shape = (blocks // 4, n, wide)
    out_specs = [pl.BlockSpec((blocks, n, s), lambda i: (0, 0, chunk)), whole((slots, n, s))]
    out_shape = [jax.ShapeDtypeStruct(cot.shape, F32), jax.ShapeDtypeStruct((slots, n, s), F32)]
    scratch = [
        pltpu.VMEM((prods, n, s), F32),
        pltpu.VMEM((prods, 8, s), F32),
        pltpu.VMEM((prods, n, s), F32),
        pltpu.VMEM((wide, 2 * s), BF16),
    ]
    aliases = {}
    if last:
        in_specs += [ANY, whole(flow_shape)]
        args += [top, before]
        aliases = {len(args) - 2: 0}
        out_specs += [ANY] * 4
        out_shape += [jax.ShapeDtypeStruct(part_shape, F32)] * 4
        scratch += [pltpu.VMEM(flow_shape, F32), pltpu.SemaphoreType.DMA((4,))]
    else:
        out_specs += [whole(flow_shape)]
        out_shape += [jax.ShapeDtypeStruct(flow_shape, F32)]
    return pl.pallas_call(
        functools.partial(middle_kernel, kids, last),
        grid=(1,),
        in_specs=in_specs,
        out_specs=out_specs,
        out_shape=out_shape,
        scratch_shapes=scratch,
        input_output_aliases=aliases,
        name="middle",
        cost_estimate=cost(6 * blocks * 2 * n * wide * 2 * s, 14 << 20),
    )(*args)


def flow_kernel(kids, last, me_ref, sums_ref, ids_ref, recv_ref, e_ref, m_ref, tot_ref, *refs):
    if last:
        before_ref, ratio_ref, f0, f1, f2, f3, x_ref, flow_ref, sem = refs
    else:
        ratio_ref, flow_ref, x_ref = refs
    blocks, n, s = tot_ref.shape
    home_sums(ids_ref, recv_ref, ratio_ref)

    def body(at, carry):
        b = lax.rem(at + me_ref[0], blocks)
        _, factors = scales(sums_ref, b, kids, m_ref)
        fill_terms(sums_ref, b, kids, e_ref, factors, x_ref)
        ratio = ratio_ref[b] / tot_ref[b]
        ratio_ref[b] = ratio
        r_high, r_low = split(ratio)
        flow = weight_terms(r_high, r_low, x_ref, s)
        flow_ref[at] = flow + before_ref[at] if last else flow
        return carry

    lax.fori_loop(0, blocks, body, 0)
    if last:
        part = blocks // 4
        outs = (f0, f1, f2, f3)
        for j in range(4):
            pltpu.make_async_copy(flow_ref.at[pl.ds(j * part, part)], outs[j], sem.at[j]).start()
        for j in range(4):
            pltpu.make_async_copy(flow_ref.at[pl.ds(j * part, part)], outs[j], sem.at[j]).wait()


def flow_layer(me, sum_ids, ids, recv, e, m, totals, before=None):
    slots, n, s = recv.shape
    blocks = totals.shape[0]
    prods = e.shape[0]
    kids = sum_ids.shape[0] // blocks
    wide = kids * n
    last = before is not None
    flow_shape = (blocks, n, wide)
    part_shape = (blocks // 4, n, wide)
    in_specs = [
        SMEM,
        SMEM,
        SMEM,
        whole((slots, n, s)),
        whole((prods, n, s)),
        whole((prods, 8, s)),
        whole((blocks, n, s)),
    ]
    args = [me, sum_ids, ids, recv, e, m, totals]
    out_specs = [whole((blocks, n, s))]
    out_shape = [jax.ShapeDtypeStruct((blocks, n, s), F32)]
    scratch = [pltpu.VMEM((wide, 2 * s), BF16)]
    if last:
        in_specs += [whole(flow_shape)]
        args += [before]
        out_specs += [ANY] * 4
        out_shape += [jax.ShapeDtypeStruct(part_shape, F32)] * 4
        scratch += [pltpu.VMEM(flow_shape, F32), pltpu.SemaphoreType.DMA((4,))]
    else:
        out_specs += [whole(flow_shape)]
        out_shape += [jax.ShapeDtypeStruct(flow_shape, F32)]
    return pl.pallas_call(
        functools.partial(flow_kernel, kids, last),
        grid=(1,),
        in_specs=in_specs,
        out_specs=out_specs,
        out_shape=out_shape,
        scratch_shapes=scratch,
        name="flow",
        cost_estimate=cost(2 * blocks * 2 * n * wide * 2 * s, 10 << 20),
    )(*args)


def backward_kernel(kids, kids_ref, sums_ref, ratio_ref, e_ref, m_ref, wt_ref, sg_ref, g_ref):
    g_ref[...] = jnp.zeros_like(g_ref)

    def body(b, carry):
        _, factors = scales(sums_ref, b, kids, m_ref)
        r_high, r_low = split(ratio_ref[b])
        child_terms(wt_ref[0, b], r_high, r_low, sums_ref, b, kids, factors, g_ref)
        return carry

    lax.fori_loop(0, ratio_ref.shape[0], body, 0)
    slot_terms(kids_ref, e_ref, g_ref, sg_ref)


def backward_layer(layer, slots, kids_ids, sum_ids, ratio, e, m, wt):
    blocks, n, s = ratio.shape
    prods = e.shape[0]
    wide = wt.shape[2]
    return pl.pallas_call(
        functools.partial(backward_kernel, wide // n),
        grid=(1,),
        in_specs=[
            SMEM,
            SMEM,
            whole((blocks, n, s)),
            whole((prods, n, s)),
            whole((prods, 8, s)),
            pl.BlockSpec((1, blocks, wide, 2 * n), lambda i: (layer, 0, 0, 0)),
        ],
        out_specs=whole((slots, n, s)),
        out_shape=jax.ShapeDtypeStruct((slots, n, s), F32),
        scratch_shapes=[pltpu.VMEM((prods, n, s), F32)],
        name="backward",
        cost_estimate=cost(2 * blocks * 2 * n * wide * 2 * s, 8 << 20),
    )(kids_ids, sum_ids, ratio, e, m, wt)


def home_kernel(ids_ref, recv_ref, *refs):
    home_sums(ids_ref, recv_ref, refs[-1])


def home(ids, recv, chunk, shape, into=None):
    slots, n, s = recv.shape
    blocks = shape[0]
    args = [ids, recv]
    in_specs = [SMEM, whole((slots, n, s))]
    aliases = {}
    if into is not None:
        args += [into]
        in_specs += [ANY]
        aliases = {2: 0}
    return pl.pallas_call(
        home_kernel,
        grid=(1,),
        in_specs=in_specs,
        out_specs=pl.BlockSpec((blocks, n, s), lambda i: (0, 0, chunk)),
        out_shape=jax.ShapeDtypeStruct(shape, F32),
        input_output_aliases=aliases,
        name="home",
        cost_estimate=cost(0, 3 << 20),
    )(*args)


def format_kernel(kids, me_ref, q0, q1, q2, q3, *refs):
    out_ref = refs[-1]
    n = q0.shape[1]
    for j, q in enumerate((q0, q1, q2, q3)):

        @pl.when(pl.program_id(0) == j)
        def _(q=q):
            for i in range(q.shape[0]):
                for k in range(kids):
                    out_ref[0, i, k] = q[i, :, k * n : (k + 1) * n]


def format_flow(layer, me, quarters, shape, into=None):
    part, n, wide = quarters[0].shape
    kids = wide // n
    args = [me, *quarters]
    in_specs = [pl.BlockSpec((part, n, wide), lambda j, me_ref: (0, 0, 0))] * 4
    aliases = {}
    if into is not None:
        args += [into]
        in_specs += [ANY]
        aliases = {5: 0}
    return pl.pallas_call(
        functools.partial(format_kernel, kids),
        grid_spec=pltpu.PrefetchScalarGridSpec(
            num_scalar_prefetch=1,
            grid=(4,),
            in_specs=in_specs,
            out_specs=pl.BlockSpec(
                (1, part, kids, n, n),
                lambda j, me_ref: (layer, lax.rem(me_ref[0] // part + j, 4), 0, 0, 0),
            ),
        ),
        out_shape=jax.ShapeDtypeStruct(shape, F32),
        input_output_aliases=aliases,
        name="format",
        cost_estimate=cost(0, 6 << 20),
    )(*args)


def exchange(parts):
    return [
        lax.ppermute(part, "dp", [(d, (d + j) % 4) for d in range(4)])
        for j, part in enumerate(parts, start=1)
    ]


def reduce_flow(parts, samples):
    own, *others = parts
    got = exchange(others)
    total = (own + got[0] + got[1] + got[2]) * (1.0 / samples)
    back, across, ahead = exchange([total] * 3)
    return [total, ahead, across, back]


def per_device(leaves, weights, groups, prod_kids, sum_kids, cotangent):
    levels, blocks = weights.shape[:2]
    per = leaves.shape[2]
    s = 128
    chunks = per // s
    samples_all = per * lax.axis_size("dp")
    ids = [groups[l].reshape(-1) for l in range(levels)]
    kids_ids = [prod_kids[l].reshape(-1) for l in range(levels)]
    sum_ids = [sum_kids[l].reshape(-1) for l in range(levels)]
    me = (lax.axis_index("dp") * (blocks // 4)).astype(jnp.int32).reshape(1)
    slots = ids[0].shape[0]
    wf, wt = prepare(weights)

    def swap(x):
        return lax.all_to_all(x, "region", split_axis=0, concat_axis=0, tiled=True)

    span = range(chunks)
    got = [swap(take(ids[0], leaves, c, s)) for c in span]
    kept = []
    for c in span:
        sent, *rest = forward_layer(0, kids_ids[0], sum_ids[0], ids[1], got[c], wf)
        got[c] = swap(sent)
        kept.append(rest)
    top = before = None
    for c in span:
        if c == 0:
            top, sent, before = middle_layer(1, c, me, kids_ids[1], sum_ids[1], got[c], cotangent, wf, wt)
        else:
            top, sent, *parts_1 = middle_layer(
                1, c, me, kids_ids[1], sum_ids[1], got[c], cotangent, wf, wt, top, before
            )
        got[c] = swap(sent)
    flow_1 = reduce_flow(parts_1, samples_all)
    before = None
    for c in span:
        e, m, totals = kept[c]
        if c == 0:
            ratio, before = flow_layer(me, sum_ids[0], ids[1], got[c], e, m, totals)
        else:
            ratio, *parts_0 = flow_layer(me, sum_ids[0], ids[1], got[c], e, m, totals, before)
        got[c] = swap(backward_layer(0, slots, kids_ids[0], sum_ids[0], ratio, e, m, wt))
    flow_0 = reduce_flow(parts_0, samples_all)
    leaf_grad = None
    for c in span:
        leaf_grad = home(ids[0], got[c], c, leaves.shape, leaf_grad)
    weight_flow = format_flow(1, me, flow_1, weights.shape)
    weight_flow = format_flow(0, me, flow_0, weights.shape, weight_flow)
    return top, leaf_grad, weight_flow


def solution(mesh):
    placed = (
        P("region", None, "dp"),
        P(None, "region", None, None, None),
        P(None, None, "region", None),
        P(None, "region", None),
        P(None, "region", None),
        P("region", None, "dp"),
    )
    return jax.shard_map(
        per_device,
        mesh=mesh,
        in_specs=placed,
        out_specs=(
            P("region", None, "dp"),
            P("region", None, "dp"),
            P(None, "region", None, None, None),
        ),
        check_vma=False,
    )
```

```python
import functools

import jax
import jax.numpy as jnp
from jax import lax
from jax.experimental import pallas as pl
from jax.experimental.pallas import tpu as pltpu
from jax.sharding import PartitionSpec as P


F32 = jnp.float32
BF16 = jnp.bfloat16
ANY = pl.BlockSpec(memory_space=pl.ANY)
SMEM = pl.BlockSpec(memory_space=pltpu.SMEM)
HBM = pl.BlockSpec(memory_space=pltpu.HBM)
PARAMS = pltpu.CompilerParams(vmem_limit_bytes=67043328)


def whole(shape):
    return pl.BlockSpec(shape, lambda i: (0,) * len(shape))


def cost(flops, touched):
    return pl.CostEstimate(flops=flops, bytes_accessed=touched, transcendentals=0)


def split(x):
    high = x.astype(BF16)
    return high, (x - high.astype(F32)).astype(BF16)


def prepare_kernel(w_ref, wf_ref, wt_ref):
    kids = w_ref.shape[2]
    wide = jnp.concatenate([w_ref[0, 0, k] for k in range(kids)], axis=1)
    high = wide.astype(BF16)
    low = (wide - high.astype(F32)).astype(BF16)
    stacked = jnp.concatenate([high, low], axis=0)
    wf_ref[0, 0] = stacked
    both = jnp.concatenate([high.astype(F32), low.astype(F32)], axis=0)
    wt_ref[0, 0] = both.T.astype(BF16)


def prepare(weights):
    levels, blocks, kids, n, _ = weights.shape
    return pl.pallas_call(
        prepare_kernel,
        grid=(levels, blocks),
        in_specs=[pl.BlockSpec((1, 1, kids, n, n), lambda l, b: (l, b, 0, 0, 0))],
        out_specs=[
            pl.BlockSpec((1, 1, 2 * n, kids * n), lambda l, b: (l, b, 0, 0)),
            pl.BlockSpec((1, 1, kids * n, 2 * n), lambda l, b: (l, b, 0, 0)),
        ],
        out_shape=[
            jax.ShapeDtypeStruct((levels, blocks, 2 * n, kids * n), BF16),
            jax.ShapeDtypeStruct((levels, blocks, kids * n, 2 * n), BF16),
        ],
        name="prepare",
        compiler_params=PARAMS,
        cost_estimate=cost(0, 20 << 20),
    )(weights)


def send_slots(ids_ref, source, out_ref, sem):
    count = out_ref.shape[0]

    def start(t, carry):
        pltpu.make_async_copy(source.at[ids_ref[t]], out_ref.at[t], sem.at[t]).start()
        return carry

    def finish(t, carry):
        pltpu.make_async_copy(source.at[0], out_ref.at[t], sem.at[t]).wait()
        return carry

    lax.fori_loop(0, count, start, 0)
    lax.fori_loop(0, count, finish, 0)


def take_kernel(ids_ref, leaves_ref, out_ref, sem):
    send_slots(ids_ref, leaves_ref, out_ref, sem)


def take(ids, leaves, chunk, s):
    blocks, n, _ = leaves.shape
    slots = ids.shape[0]
    return pl.pallas_call(
        take_kernel,
        grid=(1,),
        in_specs=[SMEM, pl.BlockSpec((blocks, n, s), lambda i: (0, 0, chunk))],
        out_specs=ANY,
        out_shape=jax.ShapeDtypeStruct((slots, n, s), F32),
        scratch_shapes=[pltpu.SemaphoreType.DMA((slots,))],
        name="take",
        compiler_params=PARAMS,
        cost_estimate=cost(0, 6 << 20),
    )(ids, leaves)


def fetch(source, into, sem):
    parts = sem.shape[0]
    rows = source.shape[0] // parts
    copies = [
        pltpu.make_async_copy(source.at[pl.ds(i * rows, rows)], into.at[pl.ds(i * rows, rows)], sem.at[i])
        for i in range(parts)
    ]
    for copy in copies:
        copy.start()
    for copy in copies:
        copy.wait()


def fetch_scratch(slots, n, s):
    return [pltpu.VMEM((slots, n, s), F32), pltpu.SemaphoreType.DMA((8,))]


def make_products(kids_ref, recv_ref, e_ref, m_ref):
    n, s = recv_ref.shape[1:]

    def body(p, carry):
        prod = recv_ref[kids_ref[2 * p]] + recv_ref[kids_ref[2 * p + 1]]
        top = jnp.broadcast_to(jnp.max(prod, axis=0, keepdims=True), (8, s))
        m_ref[p] = top
        e_ref[p] = jnp.exp(prod.reshape(n // 8, 8, s) - top[None]).reshape(n, s)
        return carry

    lax.fori_loop(0, e_ref.shape[0], body, 0, unroll=2)


def scales(sums_ref, b, kids, m_ref):
    tops = [m_ref[sums_ref[b * kids + k]] for k in range(kids)]
    shift = functools.reduce(jnp.maximum, tops)
    return shift, [jnp.exp(t - shift) for t in tops]


def fill_terms(sums_ref, b, kids, e_ref, factors, x_ref):
    n, s = e_ref.shape[1:]
    for k in range(kids):
        e = e_ref[sums_ref[b * kids + k]]
        high, low = split((e.reshape(n // 8, 8, s) * factors[k][None]).reshape(n, s))
        x_ref[pl.ds(k * n, n), pl.ds(0, s)] = high
        x_ref[pl.ds(k * n, n), pl.ds(s, s)] = low


def sum_terms(wf, x_ref, n, s):
    both = jnp.dot(wf, x_ref[...], preferred_element_type=F32)
    return (both[:n, :s] + (both[n:, :s] + both[:n, s:])) + both[n:, s:]


def add_shift(shift, totals):
    n, s = totals.shape
    return (jnp.log(totals).reshape(n // 8, 8, s) + shift[None]).reshape(n, s)


def weight_terms(r_high, r_low, x_ref, s):
    dims = (((1,), (1,)), ((), ()))
    main = lax.dot_general(
        jnp.concatenate([r_high, r_high], axis=1), x_ref[...], dims, preferred_element_type=F32
    )
    return main + lax.dot_general(
        r_low, x_ref[:, pl.ds(0, s)], dims, preferred_element_type=F32
    )


def child_terms(wt, r_high, r_low, sums_ref, b, kids, factors, g_ref):
    n, s = r_high.shape
    right = jnp.concatenate([r_high, r_high, r_low, r_low], axis=0)
    y = jnp.dot(jnp.concatenate([wt, wt], axis=1), right, preferred_element_type=F32)
    for k in range(kids):
        p = sums_ref[b * kids + k]
        part = y[k * n : (k + 1) * n].reshape(n // 8, 8, s) * factors[k][None]
        g_ref[p] = g_ref[p] + part.reshape(n, s)


def slot_terms(kids_ref, e_ref, g_ref, out_ref):
    out_ref[...] = jnp.zeros_like(out_ref)

    def body(p, carry):
        g = g_ref[p] * e_ref[p]
        first, second = kids_ref[2 * p], kids_ref[2 * p + 1]
        out_ref[first] = out_ref[first] + g
        out_ref[second] = out_ref[second] + g
        return carry

    lax.fori_loop(0, e_ref.shape[0], body, 0)


def home_sums(ids_ref, recv_ref, acc_ref):
    acc_ref[...] = jnp.zeros_like(acc_ref)

    def body(t, carry):
        b = ids_ref[t]
        acc_ref[b] = acc_ref[b] + recv_ref[t]
        return carry

    lax.fori_loop(0, recv_ref.shape[0], body, 0)


def forward_kernel(kids, kids_ref, sums_ref, next_ref, recv_hbm, wf_ref, out_ref, e_ref, m_ref, tot_ref, recv_ref, recv_sem, lv_ref, x_ref, sem):
    n, s = recv_ref.shape[1:]
    fetch(recv_hbm, recv_ref, recv_sem)
    make_products(kids_ref, recv_ref, e_ref, m_ref)

    def body(b, carry):
        shift, factors = scales(sums_ref, b, kids, m_ref)
        fill_terms(sums_ref, b, kids, e_ref, factors, x_ref)
        totals = sum_terms(wf_ref[0, b], x_ref, n, s)
        tot_ref[b] = totals
        lv_ref[b] = add_shift(shift, totals)
        return carry

    lax.fori_loop(0, lv_ref.shape[0], body, 0)
    send_slots(next_ref, lv_ref, out_ref, sem)


def forward_layer(layer, kids_ids, sum_ids, next_ids, recv, wf):
    slots, n, s = recv.shape
    blocks, _, wide = wf.shape[1:]
    kids = wide // n
    prods = kids_ids.shape[0] // 2
    return pl.pallas_call(
        functools.partial(forward_kernel, kids),
        grid=(1,),
        in_specs=[
            SMEM,
            SMEM,
            SMEM,
            HBM,
            pl.BlockSpec((1, blocks, 2 * n, wide), lambda i: (layer, 0, 0, 0)),
        ],
        out_specs=[ANY, whole((prods, n, s)), whole((prods, 8, s)), whole((blocks, n, s))],
        out_shape=[
            jax.ShapeDtypeStruct((slots, n, s), F32),
            jax.ShapeDtypeStruct((prods, n, s), F32),
            jax.ShapeDtypeStruct((prods, 8, s), F32),
            jax.ShapeDtypeStruct((blocks, n, s), F32),
        ],
        scratch_shapes=[
            *fetch_scratch(slots, n, s),
            pltpu.VMEM((blocks, n, s), F32),
            pltpu.VMEM((wide, 2 * s), BF16),
            pltpu.SemaphoreType.DMA((slots,)),
        ],
        name="forward",
        compiler_params=PARAMS,
        cost_estimate=cost(2 * blocks * 2 * n * wide * 2 * s, 10 << 20),
    )(kids_ids, sum_ids, next_ids, recv, wf)


def middle_kernel(kids, last, me_ref, kids_ref, sums_ref, recv_hbm, cot_ref, wf_ref, wt_ref, *refs):
    if last:
        _, before_ref, top_ref, sg_ref, f0, f1, f2, f3, recv_ref, recv_sem, e_ref, m_ref, g_ref, x_ref, flow_ref, sem = refs
    else:
        top_ref, sg_ref, flow_ref, recv_ref, recv_sem, e_ref, m_ref, g_ref, x_ref = refs
    fetch(recv_hbm, recv_ref, recv_sem)
    n, s = recv_ref.shape[1:]
    blocks = cot_ref.shape[0]
    make_products(kids_ref, recv_ref, e_ref, m_ref)
    g_ref[...] = jnp.zeros_like(g_ref)

    def body(at, carry):
        b = lax.rem(at + me_ref[0], blocks)
        shift, factors = scales(sums_ref, b, kids, m_ref)
        fill_terms(sums_ref, b, kids, e_ref, factors, x_ref)
        totals = sum_terms(wf_ref[0, b], x_ref, n, s)
        top_ref[b] = add_shift(shift, totals)
        r_high, r_low = split(cot_ref[b] / totals)
        flow = weight_terms(r_high, r_low, x_ref, s)
        flow_ref[at] = flow + before_ref[at] if last else flow
        child_terms(wt_ref[0, b], r_high, r_low, sums_ref, b, kids, factors, g_ref)
        return carry

    lax.fori_loop(0, blocks, body, 0)
    if last:
        part = blocks // 4
        outs = (f0, f1, f2, f3)
        for j in range(4):
            pltpu.make_async_copy(flow_ref.at[pl.ds(j * part, part)], outs[j], sem.at[j]).start()
    slot_terms(kids_ref, e_ref, g_ref, sg_ref)
    if last:
        for j in range(4):
            pltpu.make_async_copy(flow_ref.at[pl.ds(j * part, part)], outs[j], sem.at[j]).wait()


def middle_layer(layer, chunk, me, kids_ids, sum_ids, recv, cot, wf, wt, top=None, before=None):
    slots, n, s = recv.shape
    blocks, _, wide = wf.shape[1:]
    kids = wide // n
    prods = kids_ids.shape[0] // 2
    last = before is not None
    in_specs = [
        SMEM,
        SMEM,
        SMEM,
        HBM,
        pl.BlockSpec((blocks, n, s), lambda i: (0, 0, chunk)),
        pl.BlockSpec((1, blocks, 2 * n, wide), lambda i: (layer, 0, 0, 0)),
        pl.BlockSpec((1, blocks, wide, 2 * n), lambda i: (layer, 0, 0, 0)),
    ]
    args = [me, kids_ids, sum_ids, recv, cot, wf, wt]
    flow_shape = (blocks, n, wide)
    part_shape = (blocks // 4, n, wide)
    out_specs = [pl.BlockSpec((blocks, n, s), lambda i: (0, 0, chunk)), whole((slots, n, s))]
    out_shape = [jax.ShapeDtypeStruct(cot.shape, F32), jax.ShapeDtypeStruct((slots, n, s), F32)]
    scratch = [
        *fetch_scratch(slots, n, s),
        pltpu.VMEM((prods, n, s), F32),
        pltpu.VMEM((prods, 8, s), F32),
        pltpu.VMEM((prods, n, s), F32),
        pltpu.VMEM((wide, 2 * s), BF16),
    ]
    aliases = {}
    if last:
        in_specs += [ANY, whole(flow_shape)]
        args += [top, before]
        aliases = {len(args) - 2: 0}
        out_specs += [ANY] * 4
        out_shape += [jax.ShapeDtypeStruct(part_shape, F32)] * 4
        scratch += [pltpu.VMEM(flow_shape, F32), pltpu.SemaphoreType.DMA((4,))]
    else:
        out_specs += [whole(flow_shape)]
        out_shape += [jax.ShapeDtypeStruct(flow_shape, F32)]
    return pl.pallas_call(
        functools.partial(middle_kernel, kids, last),
        grid=(1,),
        in_specs=in_specs,
        out_specs=out_specs,
        out_shape=out_shape,
        scratch_shapes=scratch,
        input_output_aliases=aliases,
        name="middle",
        compiler_params=PARAMS,
        cost_estimate=cost(6 * blocks * 2 * n * wide * 2 * s, 14 << 20),
    )(*args)


def flow_kernel(kids, last, me_ref, sums_ref, ids_ref, recv_hbm, e_ref, m_ref, tot_ref, *refs):
    if last:
        before_ref, ratio_ref, f0, f1, f2, f3, recv_ref, recv_sem, x_ref, flow_ref, sem = refs
    else:
        ratio_ref, flow_ref, recv_ref, recv_sem, x_ref = refs
    fetch(recv_hbm, recv_ref, recv_sem)
    blocks, _, s = tot_ref.shape
    home_sums(ids_ref, recv_ref, ratio_ref)

    def body(at, carry):
        b = lax.rem(at + me_ref[0], blocks)
        _, factors = scales(sums_ref, b, kids, m_ref)
        fill_terms(sums_ref, b, kids, e_ref, factors, x_ref)
        ratio = ratio_ref[b] / tot_ref[b]
        ratio_ref[b] = ratio
        r_high, r_low = split(ratio)
        flow = weight_terms(r_high, r_low, x_ref, s)
        flow_ref[at] = flow + before_ref[at] if last else flow
        return carry

    lax.fori_loop(0, blocks, body, 0)
    if last:
        part = blocks // 4
        outs = (f0, f1, f2, f3)
        for j in range(4):
            pltpu.make_async_copy(flow_ref.at[pl.ds(j * part, part)], outs[j], sem.at[j]).start()
        for j in range(4):
            pltpu.make_async_copy(flow_ref.at[pl.ds(j * part, part)], outs[j], sem.at[j]).wait()


def flow_layer(me, sum_ids, ids, recv, e, m, totals, before=None):
    slots, n, s = recv.shape
    blocks = totals.shape[0]
    prods = e.shape[0]
    kids = sum_ids.shape[0] // blocks
    wide = kids * n
    last = before is not None
    flow_shape = (blocks, n, wide)
    part_shape = (blocks // 4, n, wide)
    in_specs = [
        SMEM,
        SMEM,
        SMEM,
        HBM,
        whole((prods, n, s)),
        whole((prods, 8, s)),
        whole((blocks, n, s)),
    ]
    args = [me, sum_ids, ids, recv, e, m, totals]
    out_specs = [whole((blocks, n, s))]
    out_shape = [jax.ShapeDtypeStruct((blocks, n, s), F32)]
    scratch = [*fetch_scratch(slots, n, s), pltpu.VMEM((wide, 2 * s), BF16)]
    if last:
        in_specs += [whole(flow_shape)]
        args += [before]
        out_specs += [ANY] * 4
        out_shape += [jax.ShapeDtypeStruct(part_shape, F32)] * 4
        scratch += [pltpu.VMEM(flow_shape, F32), pltpu.SemaphoreType.DMA((4,))]
    else:
        out_specs += [whole(flow_shape)]
        out_shape += [jax.ShapeDtypeStruct(flow_shape, F32)]
    return pl.pallas_call(
        functools.partial(flow_kernel, kids, last),
        grid=(1,),
        in_specs=in_specs,
        out_specs=out_specs,
        out_shape=out_shape,
        scratch_shapes=scratch,
        name="flow",
        compiler_params=PARAMS,
        cost_estimate=cost(2 * blocks * 2 * n * wide * 2 * s, 10 << 20),
    )(*args)


def backward_kernel(kids, kids_ref, sums_ref, ratio_ref, e_ref, m_ref, wt_ref, sg_ref, g_ref):
    g_ref[...] = jnp.zeros_like(g_ref)

    def body(b, carry):
        _, factors = scales(sums_ref, b, kids, m_ref)
        r_high, r_low = split(ratio_ref[b])
        child_terms(wt_ref[0, b], r_high, r_low, sums_ref, b, kids, factors, g_ref)
        return carry

    lax.fori_loop(0, ratio_ref.shape[0], body, 0)
    slot_terms(kids_ref, e_ref, g_ref, sg_ref)


def backward_layer(layer, slots, kids_ids, sum_ids, ratio, e, m, wt):
    blocks, n, s = ratio.shape
    prods = e.shape[0]
    wide = wt.shape[2]
    return pl.pallas_call(
        functools.partial(backward_kernel, wide // n),
        grid=(1,),
        in_specs=[
            SMEM,
            SMEM,
            whole((blocks, n, s)),
            whole((prods, n, s)),
            whole((prods, 8, s)),
            pl.BlockSpec((1, blocks, wide, 2 * n), lambda i: (layer, 0, 0, 0)),
        ],
        out_specs=whole((slots, n, s)),
        out_shape=jax.ShapeDtypeStruct((slots, n, s), F32),
        scratch_shapes=[pltpu.VMEM((prods, n, s), F32)],
        name="backward",
        compiler_params=PARAMS,
        cost_estimate=cost(2 * blocks * 2 * n * wide * 2 * s, 8 << 20),
    )(kids_ids, sum_ids, ratio, e, m, wt)


def home_kernel(ids_ref, recv_hbm, *refs):
    out_ref, recv_ref, recv_sem = refs[-3:]
    fetch(recv_hbm, recv_ref, recv_sem)
    home_sums(ids_ref, recv_ref, out_ref)


def home(ids, recv, chunk, shape, into=None):
    slots, n, s = recv.shape
    blocks = shape[0]
    args = [ids, recv]
    in_specs = [SMEM, HBM]
    aliases = {}
    if into is not None:
        args += [into]
        in_specs += [ANY]
        aliases = {2: 0}
    return pl.pallas_call(
        home_kernel,
        grid=(1,),
        in_specs=in_specs,
        out_specs=pl.BlockSpec((blocks, n, s), lambda i: (0, 0, chunk)),
        out_shape=jax.ShapeDtypeStruct(shape, F32),
        scratch_shapes=fetch_scratch(slots, n, s),
        input_output_aliases=aliases,
        name="home",
        compiler_params=PARAMS,
        cost_estimate=cost(0, 3 << 20),
    )(*args)


def format_kernel(kids, me_ref, q0, q1, q2, q3, *refs):
    out_ref = refs[-1]
    n = q0.shape[1]
    for j, q in enumerate((q0, q1, q2, q3)):

        @pl.when(pl.program_id(0) == j)
        def _(q=q):
            for i in range(q.shape[0]):
                for k in range(kids):
                    out_ref[0, i, k] = q[i, :, k * n : (k + 1) * n]


def format_flow(layer, me, quarters, shape, into=None):
    part, n, wide = quarters[0].shape
    kids = wide // n
    args = [me, *quarters]
    in_specs = [pl.BlockSpec((part, n, wide), lambda j, me_ref: (0, 0, 0))] * 4
    aliases = {}
    if into is not None:
        args += [into]
        in_specs += [ANY]
        aliases = {5: 0}
    return pl.pallas_call(
        functools.partial(format_kernel, kids),
        grid_spec=pltpu.PrefetchScalarGridSpec(
            num_scalar_prefetch=1,
            grid=(4,),
            in_specs=in_specs,
            out_specs=pl.BlockSpec(
                (1, part, kids, n, n),
                lambda j, me_ref: (layer, lax.rem(me_ref[0] // part + j, 4), 0, 0, 0),
            ),
        ),
        out_shape=jax.ShapeDtypeStruct(shape, F32),
        input_output_aliases=aliases,
        name="format",
        compiler_params=PARAMS,
        cost_estimate=cost(0, 6 << 20),
    )(*args)


def exchange(parts):
    return [
        lax.ppermute(part, "dp", [(d, (d + j) % 4) for d in range(4)])
        for j, part in enumerate(parts, start=1)
    ]


def reduce_flow(parts, samples):
    own, *others = parts
    got = exchange(others)
    total = (own + got[0] + got[1] + got[2]) * (1.0 / samples)
    back, across, ahead = exchange([total] * 3)
    return [total, ahead, across, back]


def per_device(leaves, weights, groups, prod_kids, sum_kids, cotangent):
    levels, blocks = weights.shape[:2]
    per = leaves.shape[2]
    s = 128
    chunks = per // s
    samples_all = per * lax.axis_size("dp")
    ids = [groups[l].reshape(-1) for l in range(levels)]
    kids_ids = [prod_kids[l].reshape(-1) for l in range(levels)]
    sum_ids = [sum_kids[l].reshape(-1) for l in range(levels)]
    me = (lax.axis_index("dp") * (blocks // 4)).astype(jnp.int32).reshape(1)
    slots = ids[0].shape[0]
    wf, wt = prepare(weights)

    def swap(x):
        return lax.all_to_all(x, "region", split_axis=0, concat_axis=0, tiled=True)

    span = range(chunks)
    got = []
    for c in span:
        sent = take(ids[0], leaves, c, s)
        got.append(swap(sent))
    kept = []
    for c in span:
        sent, *rest = forward_layer(0, kids_ids[0], sum_ids[0], ids[1], got[c], wf)
        got[c] = swap(sent)
        kept.append(rest)
    top = before = None
    for c in span:
        args = (1, c, me, kids_ids[1], sum_ids[1], got[c], cotangent, wf, wt)
        if c == 0:
            top, sent, before = middle_layer(*args)
        else:
            top, sent, *parts = middle_layer(*args, top, before)
        got[c] = swap(sent)
    flow_1 = reduce_flow(parts, samples_all)
    before = None
    for c in span:
        e, m, totals = kept[c]
        if c == 0:
            ratio, before = flow_layer(me, sum_ids[0], ids[1], got[c], e, m, totals)
        else:
            ratio, *parts = flow_layer(me, sum_ids[0], ids[1], got[c], e, m, totals, before)
        sent = backward_layer(0, slots, kids_ids[0], sum_ids[0], ratio, e, m, wt)
        got[c] = swap(sent)
    flow_0 = reduce_flow(parts, samples_all)
    leaf_grad = None
    for c in span:
        leaf_grad = home(ids[0], got[c], c, leaves.shape, leaf_grad)
    weight_flow = format_flow(1, me, flow_1, weights.shape)
    weight_flow = format_flow(0, me, flow_0, weights.shape, weight_flow)
    return top, leaf_grad, weight_flow


def solution(mesh):
    placed = (
        P("region", None, "dp"),
        P(None, "region", None, None, None),
        P(None, None, "region", None),
        P(None, "region", None),
        P(None, "region", None),
        P("region", None, "dp"),
    )

    return jax.shard_map(
        per_device,
        mesh=mesh,
        in_specs=placed,
        out_specs=(
            P("region", None, "dp"),
            P("region", None, "dp"),
            P(None, "region", None, None, None),
        ),
        check_vma=False,
    )
```
